32 devices in a mesh: groups: 2 (over x), ctx: 16 (over z, y, core).
Axes of the slice: x: 2, y: 2, z: 4, core: 2. Of those that a mesh axis runs over, the one named last changes fastest.
Arguments:
- queries: bfloat16 [16384, 4096], P(('groups', 'ctx')), parts along dimension 0, may hold values from -10 to 10
- keys: bfloat16 [16384, 512], P(('groups', 'ctx')), parts along dimension 0, may hold values from -6 to 6
- values: bfloat16 [16384, 512], P(('groups', 'ctx')), parts along dimension 0, may hold values from -6 to 6
- selected: int32 [32, 2], P(('groups', 'ctx')), parts along dimension 0, may hold values from 0 to 14, as said below
Outputs:
- attended: bfloat16 [16384, 4096], P(('groups', 'ctx')), parts along dimension 0
The draws below stay inside these ranges and needn't reach their ends.
There are 2 independent parts, one for each index of `groups`. The reference program is written for one: setup_inputs(seed, part) draws one part's arguments, and reference() takes and returns one part's arrays. A program takes and returns all parts, laid end to end along the dimension named above; each array names one. Nothing has to cross between parts.
Inputs may be any that keep to these rules, and one draw needn't show every extreme that they name: `selected`: row b names min(b, 2) different blocks below b; its remaining entries equal b.
All inputs are finite; a program needn't handle non-finite values.
Results may differ from the reference program's by a relative error of at most 0.0032.
Values may be sent and summed in bfloat16 or wider, within the bound.
No kernel may reach another device: no remote copies, remote signals or barrier semaphores. Data moves between devices by JAX's collectives and lax.ppermute only.
A program may use at most 128 MiB of HBM per device.

```python
import math
import jax
import jax.numpy as jnp
from jax import lax

QH = 32
KVH = 4
HD = 128
BLOCK = 512
TOPK = 2
NBLK = 16
TOKENS = 8192


def draw_queries(key, part):
    shape_full = (NBLK, BLOCK, KVH, QH // KVH, HD)
    base = 2.5 * jnp.clip(jax.random.normal(jax.random.fold_in(key, 1), shape_full, jnp.float32), -4.0, 4.0)
    return base.reshape(NBLK * BLOCK, QH * HD).astype(jnp.bfloat16)


def draw_keys(key, part):
    shape_full = (NBLK, BLOCK, KVH, HD)
    base = jnp.clip(jax.random.normal(jax.random.fold_in(key, 2), shape_full, jnp.float32), -6.0, 6.0)
    return base.reshape(NBLK * BLOCK, KVH * HD).astype(jnp.bfloat16)


def draw_selected(key, part):
    row_ids = jnp.arange(NBLK, dtype=jnp.int32)[:, None]
    col_ids = jnp.arange(NBLK, dtype=jnp.int32)[None, :]
    noise = jax.random.randint(jax.random.fold_in(key, 11), (NBLK, NBLK), 0, 1024, dtype=jnp.int32)
    boost = jax.random.randint(jax.random.fold_in(key, 12), (1, NBLK), 0, 4, dtype=jnp.int32)
    scores = (noise + 1024 * boost) * NBLK + col_ids
    forced = (row_ids == NBLK - 1) & (col_ids == NBLK - 2)
    scores = jnp.where(forced, 5 * 1024 * NBLK + col_ids, scores)
    scores = jnp.where(col_ids < row_ids, scores, -1 - col_ids)
    top_values, top_index = jax.lax.top_k(scores, TOPK)
    chosen = jnp.where(top_values >= 0, top_index.astype(jnp.int32), row_ids)
    return chosen.astype(jnp.int32)


def shard_levels(stream_key, shape, split, least, top_value):
    loudness = 1.0
    for dim, parts in split:
        draws = jax.random.uniform(jax.random.fold_in(jax.random.fold_in(stream_key, 6), dim), (parts,), jnp.float32, least / len(split), top_value / len(split))
        loudness = loudness * jnp.repeat(jnp.exp(draws), shape[dim] // parts).reshape((-1,) + (1,) * (len(shape) - 1 - dim))
    return loudness


def centred(own_key, shape, scale, most, shards=(), held_as=jnp.bfloat16):
    level = shard_levels(own_key, shape, shards, -0.22, 0.18) if shards else 1.0
    values = jax.random.normal(own_key, shape, jnp.float32) * scale * level
    return jnp.minimum(jnp.maximum(values, -most), most).astype(held_as)


def setup_inputs(seed: int = 0, part: int = 0) -> dict:
    streams_of = jax.random.split(jax.random.key(seed), 5)
    part_splits = jax.random.split(jax.random.fold_in(streams_of[4], part), 5)
    queries = draw_queries(jax.random.fold_in(jax.random.fold_in(streams_of[4], part), 71), part)
    keys = draw_keys(jax.random.fold_in(jax.random.fold_in(streams_of[4], part), 71), part)
    values = centred(part_splits[2], (TOKENS, KVH * HD), 1.0, 6.0, ((0, 16),))
    selected = draw_selected(jax.random.fold_in(jax.random.fold_in(streams_of[4], part), 71), part)
    return {"queries": queries, "keys": keys, "values": values, "selected": selected}


def reference(queries, keys, values, selected):
    group_size = QH // KVH
    scale_factor = 1.0 / math.sqrt(HD)
    query_blocks = queries.reshape(NBLK, BLOCK, KVH, group_size, HD)
    key_blocks = keys.reshape(NBLK, BLOCK, KVH, HD)
    value_blocks = values.reshape(NBLK, BLOCK, KVH, HD)
    causal = jnp.arange(BLOCK)[:, None] >= jnp.arange(BLOCK)[None, :]

    def one_block(block_index):
        chosen = selected[block_index]
        live_slots = chosen < block_index
        own_keys = lax.dynamic_index_in_dim(key_blocks, block_index, 0, keepdims=True)
        own_values = lax.dynamic_index_in_dim(value_blocks, block_index, 0, keepdims=True)
        key_set = jnp.concatenate([own_keys, jnp.take(key_blocks, chosen, axis=0)], axis=0)
        value_set = jnp.concatenate([own_values, jnp.take(value_blocks, chosen, axis=0)], axis=0)
        key_set = key_set.reshape((TOPK + 1) * BLOCK, KVH, HD).astype(jnp.float32)
        value_set = value_set.reshape((TOPK + 1) * BLOCK, KVH, HD).astype(jnp.float32)
        slot_visible = jnp.broadcast_to(jnp.repeat(live_slots, BLOCK)[None, :], (BLOCK, TOPK * BLOCK))
        visible = jnp.concatenate([causal, slot_visible], axis=1)
        query_rows = lax.dynamic_index_in_dim(query_blocks, block_index, 0, keepdims=False).astype(jnp.float32)
        scores = jnp.einsum('igqd,jgd->gqij', query_rows, key_set) * scale_factor
        scores = jnp.where(visible[None, None], scores, -1e+30)
        row_peak = lax.optimization_barrier(jnp.max(scores, axis=3, keepdims=True))
        weight = jnp.where(visible[None, None], jnp.exp(scores - row_peak), 0.0)
        row_total = lax.optimization_barrier(jnp.sum(weight, axis=3))
        rounded = lax.optimization_barrier(weight.astype(jnp.bfloat16)).astype(jnp.float32)
        mixture = jnp.einsum('gqij,jgd->igqd', rounded, value_set)
        mixture = mixture / jnp.transpose(row_total, (2, 0, 1))[:, :, :, None]
        return mixture.astype(jnp.bfloat16).reshape(BLOCK, QH * HD)
    result = lax.map(one_block, jnp.arange(NBLK, dtype=jnp.int32))
    return result.reshape(NBLK * BLOCK, QH * HD)
```

```python
import math

import jax
import jax.numpy as jnp
from jax import lax
from jax.experimental import pallas as pl
from jax.experimental.pallas import tpu as pltpu
from jax.sharding import Mesh
from jax.sharding import PartitionSpec as P


QH = 32
KVH = 4
HD = 128
BLOCK = 512
TOPK = 2
GROUP = QH // KVH
EXPONENT_SCALE = math.log2(math.e) / math.sqrt(HD)
QUERIES = 256
ONES = 16
FIRST = ((0, 1, 2, 3),)
CHUNKS = ((0,), (1,), (2,), (3,))
HEADS = 4


def attend_kernel(dead_ref, q_ref, ko_ref, vo_ref, ks_ref, vs_ref, *rest):
    out_ref, k_all, v_t = rest[-3:]

    @pl.when(pl.program_id(1) == 0)
    def _():
        k_all[:BLOCK] = ko_ref[...]
        v_t[:HD, :BLOCK] = vo_ref[...].T
        for s in range(TOPK):
            at = slice(BLOCK * (1 + s), BLOCK * (2 + s))
            k_all[at] = ks_ref[:, s].reshape(BLOCK, HD)
            v_t[:HD, at] = vs_ref[:, s].reshape(BLOCK, HD).T
        v_t[HD:, :] = jnp.ones((ONES, (TOPK + 1) * BLOCK), jnp.bfloat16)

    drop = [0.0] + [dead_ref[s] for s in range(TOPK)]

    def place(unit):
        h, r = unit
        return slice(r * QUERIES, (r + 1) * QUERIES), slice(h * HD, (h + 1) * HD)

    def scores(unit):
        own = (unit[1] + 1) * QUERIES
        spans = [(0, own)] + [(BLOCK * (1 + s), BLOCK * (2 + s)) for s in range(TOPK)]
        q = q_ref[place(unit)]
        score = [
            lax.dot_general(k_all[a:b], q, (((1,), (1,)), ((), ())), preferred_element_type=jnp.float32)
            for a, b in spans
        ]
        u = lax.broadcasted_iota(jnp.int32, (QUERIES, QUERIES), 0)
        t = lax.broadcasted_iota(jnp.int32, (QUERIES, QUERIES), 1)
        last = jnp.where(u <= t, score[0][own - QUERIES :], -1e30)
        score[0] = jnp.concatenate([score[0][: own - QUERIES], last], axis=0) if own > QUERIES else last
        return spans, score

    def finish(unit, spans, score):
        peak = jnp.max(score[0], axis=0, keepdims=True)
        for s in range(1, TOPK + 1):
            peak = jnp.maximum(peak, jnp.max(score[s], axis=0, keepdims=True) - drop[s])
        total = None
        for (a, b), x, d in zip(spans, score, drop):
            weight = jnp.exp2((x - (peak + d)) * EXPONENT_SCALE).astype(jnp.bfloat16)
            part = jnp.dot(v_t[:, a:b], weight, preferred_element_type=jnp.float32)
            total = part if total is None else total + part
        out_ref[place(unit)] = (total[:HD] / total[HD : HD + 1]).T.astype(jnp.bfloat16)

    units = [(h, r) for h in range(HEADS) for r in range(BLOCK // QUERIES)]
    current = scores(units[0])
    for at, unit in enumerate(units):
        following = scores(units[at + 1]) if at + 1 < len(units) else None
        finish(unit, *current)
        current = following


def attend(dead, queries, keys, values, arrived, heads, previous):
    count, first = len(heads), heads[0]
    sources, _, stripe, _ = arrived.shape
    steps = GROUP // HEADS
    block = (sources, TOPK, stripe, HD)
    in_specs = [
        pl.BlockSpec(memory_space=pltpu.SMEM),
        pl.BlockSpec((BLOCK, HEADS * HD), lambda g, h: (0, (first + g) * steps + h)),
        pl.BlockSpec((BLOCK, HD), lambda g, h: (0, first + g)),
        pl.BlockSpec((BLOCK, HD), lambda g, h: (0, first + g)),
        pl.BlockSpec(block, lambda g, h: (0, 0, 0, g)),
        pl.BlockSpec(block, lambda g, h: (0, 0, 0, count + g)),
    ]
    args = [dead, queries, keys, values, arrived, arrived]
    aliases = {}
    if previous is not None:
        in_specs.append(pl.BlockSpec(memory_space=pl.ANY))
        args.append(previous)
        aliases = {len(args) - 1: 0}
    pairs = BLOCK * (TOPK + 1) * BLOCK * GROUP * count
    return pl.pallas_call(
        attend_kernel,
        out_shape=jax.ShapeDtypeStruct(queries.shape, jnp.bfloat16),
        grid=(count, steps),
        in_specs=in_specs,
        out_specs=pl.BlockSpec((BLOCK, HEADS * HD), lambda g, h: (0, (first + g) * steps + h)),
        scratch_shapes=[
            pltpu.VMEM(((TOPK + 1) * BLOCK, HD), jnp.bfloat16),
            pltpu.VMEM((HD + ONES, (TOPK + 1) * BLOCK), jnp.bfloat16),
        ],
        input_output_aliases=aliases,
        cost_estimate=pl.CostEstimate(
            flops=4 * pairs * HD, transcendentals=pairs, bytes_accessed=4 * BLOCK * HD * GROUP * count
        ),
    )(*args)


def after(x, *others):
    return lax.optimization_barrier((x, *others))[0]


def whole(queries, keys, values, selected):
    peers = lax.axis_size("peer")
    stripe = BLOCK // peers
    half, peer = lax.axis_index("half"), lax.axis_index("peer")

    def exchange(x):
        return lax.all_to_all(x, "peer", split_axis=0, concat_axis=0, tiled=True)

    def columns(x, heads):
        return x[:, heads[0] * HD : (heads[-1] + 1) * HD]

    banded = []
    for heads in FIRST:
        both = jnp.concatenate([columns(keys, heads), columns(values, heads)], axis=1)
        banded.append(exchange(both.reshape(peers, stripe, both.shape[1])))
    rows = lax.broadcasted_iota(jnp.int32, (peers, TOPK), 0)
    requests = jnp.where(rows == peer, selected, 0)
    step = 1
    while step < peers:
        pairs = [(i, i ^ step) for i in range(peers)]
        requests = requests + lax.ppermute(requests, "peer", pairs)
        step *= 2
    place = jnp.where(requests // peers == half, peers, 0) + requests % peers
    place = place.reshape(-1)
    arrived = []
    lower = None
    for heads in CHUNKS:
        for group, band in zip(FIRST, banded):
            if heads[0] in group:
                n, width = len(group), HD * len(heads)
                a = (heads[0] - group[0]) * HD
                mine = jnp.concatenate([band[..., a : a + width], band[..., n * HD + a : n * HD + a + width]], axis=-1)
        if lower is not None:
            mine = after(mine, lower)
        lower = lax.ppermute(mine, "half", [(0, 1)])
        table = jnp.concatenate([lower, mine], axis=0)
        send = jnp.take(table, place, axis=0, mode="clip").reshape(peers, TOPK, stripe, table.shape[-1])
        arrived.append(exchange(send))
    block = half * peers + peer
    dead = jnp.where(selected[0] < block, 0.0, 1e30).astype(jnp.float32)
    outputs = None
    for heads, got in zip(CHUNKS, arrived):
        outputs = attend(dead, queries, keys, values, got, heads, outputs)
    return outputs


def solution(mesh):
    groups, ctx = mesh.devices.shape
    halves = 2 if ctx % 2 == 0 else 1
    inner = Mesh(mesh.devices.reshape(groups, halves, ctx // halves), ("groups", "half", "peer"))
    spec = P(("groups", "half", "peer"), None)
    return jax.shard_map(whole, mesh=inner, in_specs=(spec,) * 4, out_specs=spec, check_vma=False)
```

```python
import math

import jax
import jax.numpy as jnp
from jax import lax
from jax.experimental import pallas as pl
from jax.experimental.pallas import tpu as pltpu
from jax.sharding import Mesh
from jax.sharding import PartitionSpec as P


QH = 32
KVH = 4
HD = 128
BLOCK = 512
TOPK = 2
GROUP = QH // KVH
EXPONENT_SCALE = math.log2(math.e) / math.sqrt(HD)
QUERIES = 512
ONES = 16
KEPT = HD + 8
DIGIT = 128
CHUNKS = ((0, 1), (2, 3))
HEADS = 4
STAGED = False
NT = (((1,), (1,)), ((), ()))


def piece(unit):
    h, r = unit
    return slice(r * QUERIES, (r + 1) * QUERIES), slice(h * HD, (h + 1) * HD)


def staggered(units, scores, weigh, finish):
    scored, weighed = {}, {}
    for at in range(len(units) + 2):
        for c in "SEA":
            if c == "S" and at < len(units):
                scored[at] = scores(units[at])
            if c == "E" and 0 <= at - 1 < len(units):
                weighed[at - 1] = weigh(units[at - 1], scored.pop(at - 1))
            if c == "A" and 0 <= at - 2 < len(units):
                finish(units[at - 2], weighed.pop(at - 2))


def units_of(heads):
    return [(h, r) for h in range(heads) for r in range(BLOCK // QUERIES)]


def own_kernel(q_ref, k_ref, v_ref, kept_ref, v_t):
    @pl.when(pl.program_id(1) == 0)
    def _():
        v_t[:HD] = v_ref[...].T
        v_t[HD:] = jnp.ones((ONES, BLOCK), jnp.bfloat16)

    def scores(unit):
        own = (unit[1] + 1) * QUERIES
        x = lax.dot_general(k_ref[:own], q_ref[piece(unit)], NT, preferred_element_type=jnp.float32)
        u = lax.broadcasted_iota(jnp.int32, (QUERIES, QUERIES), 0)
        t = lax.broadcasted_iota(jnp.int32, (QUERIES, QUERIES), 1)
        last = jnp.where(u <= t, x[own - QUERIES :], -1e30)
        return jnp.concatenate([x[: own - QUERIES], last], axis=0) if own > QUERIES else last

    def weigh(unit, x):
        peak = jnp.max(x, axis=0, keepdims=True)
        return peak, jnp.exp2((x - peak) * EXPONENT_SCALE).astype(jnp.bfloat16)

    def finish(unit, held):
        h, r = unit
        peak, weight = held
        total = jnp.dot(v_t[:, : weight.shape[0]], weight, preferred_element_type=jnp.float32)
        at = slice(r * QUERIES, (r + 1) * QUERIES)
        kept_ref[h, :HD, at] = total[:HD]
        row = lax.broadcasted_iota(jnp.int32, (KEPT - HD, QUERIES), 0)
        kept_ref[h, HD:, at] = jnp.where(row == 0, total[HD : HD + KEPT - HD], peak)

    staggered(units_of(HEADS), scores, weigh, finish)


def attend_own(queries, keys, values):
    steps = GROUP // HEADS
    pairs = BLOCK * BLOCK * QH
    return pl.pallas_call(
        own_kernel,
        out_shape=jax.ShapeDtypeStruct((QH, KEPT, BLOCK), jnp.float32),
        grid=(KVH, steps),
        in_specs=[
            pl.BlockSpec((BLOCK, HEADS * HD), lambda g, h: (0, g * steps + h)),
            pl.BlockSpec((BLOCK, HD), lambda g, h: (0, g)),
            pl.BlockSpec((BLOCK, HD), lambda g, h: (0, g)),
        ],
        out_specs=pl.BlockSpec((HEADS, KEPT, BLOCK), lambda g, h: (g * steps + h, 0, 0)),
        scratch_shapes=[pltpu.VMEM((HD + ONES, BLOCK), jnp.bfloat16)],
        cost_estimate=pl.CostEstimate(
            flops=4 * pairs * HD, transcendentals=pairs, bytes_accessed=4 * QH * KEPT * BLOCK
        ),
        name="attend_own",
    )(queries, keys, values)


def slots_kernel(dead_ref, q_ref, kept_ref, ks_ref, vs_ref, *rest):
    out_ref, k_all, v_t = rest[-3:]

    @pl.when(pl.program_id(0) == 0)
    def _():
        for s in range(TOPK):
            at = slice(BLOCK * s, BLOCK * (s + 1))
            k_all[at] = ks_ref[:, s].reshape(BLOCK, HD)
            v_t[:HD, at] = vs_ref[:, s].reshape(BLOCK, HD).T
        v_t[HD:] = jnp.ones((ONES, TOPK * BLOCK), jnp.bfloat16)

    drop = [dead_ref[s] for s in range(TOPK)]
    spans = [(BLOCK * s, BLOCK * (s + 1)) for s in range(TOPK)]

    def scores(unit):
        q = q_ref[piece(unit)]
        return [lax.dot_general(k_all[a:b], q, NT, preferred_element_type=jnp.float32) for a, b in spans]

    def weigh(unit, score):
        h, r = unit
        mine = kept_ref[h, HD + 1 : HD + 2, r * QUERIES : (r + 1) * QUERIES]
        peak = mine
        for x, d in zip(score, drop):
            peak = jnp.maximum(peak, jnp.max(x, axis=0, keepdims=True) - d)
        shrink = jnp.exp2((mine - peak) * EXPONENT_SCALE)
        weights = [
            jnp.exp2((x - (peak + d)) * EXPONENT_SCALE).astype(jnp.bfloat16) for x, d in zip(score, drop)
        ]
        return shrink, weights

    def finish(unit, held):
        h, r = unit
        at = slice(r * QUERIES, (r + 1) * QUERIES)
        shrink, weights = held
        total = None
        for (a, b), weight in zip(spans, weights):
            part = jnp.dot(v_t[:, a:b], weight, preferred_element_type=jnp.float32)
            total = part if total is None else total + part
        mixture = kept_ref[h, :HD, at] * shrink + total[:HD]
        row_total = kept_ref[h, HD : HD + 1, at] * shrink + total[HD : HD + 1]
        out_ref[piece(unit)] = (mixture * (1.0 / row_total)).T.astype(jnp.bfloat16)

    staggered(units_of(HEADS), scores, weigh, finish)


def attend_slots(dead, queries, kept, arrived, head, at, previous):
    sources, _, stripe, width = arrived.shape
    count = width // (2 * HD)
    steps = GROUP // HEADS
    block = (sources, TOPK, stripe, HD)
    in_specs = [
        pl.BlockSpec(memory_space=pltpu.SMEM),
        pl.BlockSpec((BLOCK, HEADS * HD), lambda h: (0, head * steps + h)),
        pl.BlockSpec((HEADS, KEPT, BLOCK), lambda h: (head * steps + h, 0, 0)),
        pl.BlockSpec(block, lambda h: (0, 0, 0, at)),
        pl.BlockSpec(block, lambda h: (0, 0, 0, count + at)),
    ]
    args = [dead, queries, kept, arrived, arrived]
    aliases = {}
    if previous is not None:
        in_specs.append(pl.BlockSpec(memory_space=pl.ANY))
        args.append(previous)
        aliases = {len(args) - 1: 0}
    pairs = BLOCK * TOPK * BLOCK * GROUP
    return pl.pallas_call(
        slots_kernel,
        out_shape=jax.ShapeDtypeStruct(queries.shape, jnp.bfloat16),
        grid=(steps,),
        in_specs=in_specs,
        out_specs=pl.BlockSpec((BLOCK, HEADS * HD), lambda h: (0, head * steps + h)),
        scratch_shapes=[
            pltpu.VMEM((TOPK * BLOCK, HD), jnp.bfloat16),
            pltpu.VMEM((HD + ONES, TOPK * BLOCK), jnp.bfloat16),
        ],
        input_output_aliases=aliases,
        cost_estimate=pl.CostEstimate(
            flops=4 * pairs * HD, transcendentals=pairs, bytes_accessed=8 * BLOCK * HD * GROUP
        ),
    )(*args)


def after(x, *others):
    return lax.optimization_barrier((x, *others))[0]


def whole(queries, keys, values, selected):
    halves, peers = lax.axis_size("half"), lax.axis_size("peer")
    stripe = BLOCK // peers
    half, peer = lax.axis_index("half"), lax.axis_index("peer")

    def exchange(x):
        return lax.all_to_all(x, "peer", split_axis=0, concat_axis=0, tiled=True)

    def columns(x, heads):
        return x[:, heads[0] * HD : (heads[-1] + 1) * HD]

    digits = jnp.concatenate([selected // DIGIT, selected % DIGIT], axis=1).astype(jnp.bfloat16)
    banded = []
    for at, heads in enumerate(CHUNKS):
        both = jnp.concatenate([columns(keys, heads), columns(values, heads)], axis=1)
        both = both.reshape(peers, stripe, both.shape[1])
        if at == 0:
            asked = jnp.pad(digits, ((0, 15), (0, both.shape[2] - 2 * TOPK)))
            both = jnp.concatenate([both, jnp.broadcast_to(asked, (peers, *asked.shape))], axis=1)
        else:
            both = after(both, banded[0]) if STAGED else both
        banded.append(exchange(both))
    kept = attend_own(queries, keys, values)
    digits = banded[0][:, stripe, : 2 * TOPK].astype(jnp.int32)
    requests = digits[:, :TOPK] * DIGIT + digits[:, TOPK:]
    place = jnp.where(requests // peers == half, peers, 0) + requests % peers
    place = place.reshape(-1)
    arrived = []
    lower = None
    for band in banded:
        mine = band[:, :stripe]
        if lower is not None:
            mine = after(mine, lower)
        lower = lax.ppermute(mine, "half", [(0, 1)]) if halves > 1 else mine
        table = jnp.concatenate([lower, mine], axis=0)
        send = jnp.take(table, place, axis=0, mode="clip").reshape(peers, TOPK, *mine.shape[1:])
        arrived.append(exchange(send))
    block = half * peers + peer
    dead = jnp.where(selected[0] < block, 0.0, 1e30).astype(jnp.float32)
    outputs = None
    for heads, got in zip(CHUNKS, arrived):
        for at, head in enumerate(heads):
            outputs = attend_slots(dead, queries, kept, got, head, at, outputs)
    return outputs


def solution(mesh):
    groups, ctx = mesh.devices.shape
    halves = 2 if ctx % 2 == 0 else 1
    inner = Mesh(mesh.devices.reshape(groups, halves, ctx // halves), ("groups", "half", "peer"))
    spec = P(("groups", "half", "peer"), None)
    return jax.shard_map(whole, mesh=inner, in_specs=(spec,) * 4, out_specs=spec, check_vma=False)
```

```python
import math

import jax
import jax.numpy as jnp
from jax import lax
from jax.experimental import pallas as pl
from jax.experimental.pallas import tpu as pltpu
from jax.sharding import Mesh
from jax.sharding import PartitionSpec as P


QH = 32
KVH = 4
HD = 128
BLOCK = 512
TOPK = 2
GROUP = QH // KVH
EXPONENT_SCALE = math.log2(math.e) / math.sqrt(HD)
QUERIES = 512
ONES = 16
KEPT = HD + 8
DIGIT = 128
CHUNKS = ((0, 1), (2, 3))
HEADS = 4
NT = (((1,), (1,)), ((), ()))


def piece(unit):
    h, r = unit
    return slice(r * QUERIES, (r + 1) * QUERIES), slice(h * HD, (h + 1) * HD)


def staggered(units, scores, weigh, finish):
    scored, weighed = {}, {}
    for at in range(len(units) + 2):
        for c in "SEA":
            if c == "S" and at < len(units):
                scored[at] = scores(units[at])
            if c == "E" and 0 <= at - 1 < len(units):
                weighed[at - 1] = weigh(units[at - 1], scored.pop(at - 1))
            if c == "A" and 0 <= at - 2 < len(units):
                finish(units[at - 2], weighed.pop(at - 2))


def units_of(heads):
    return [(h, r) for h in range(heads) for r in range(BLOCK // QUERIES)]


def own_kernel(q_ref, k_ref, v_ref, kept_ref, v_t):
    @pl.when(pl.program_id(1) == 0)
    def _():
        v_t[:HD] = v_ref[...].T
        v_t[HD:] = jnp.ones((ONES, BLOCK), jnp.bfloat16)

    def scores(unit):
        own = (unit[1] + 1) * QUERIES
        x = lax.dot_general(k_ref[:own], q_ref[piece(unit)], NT, preferred_element_type=jnp.float32)
        u = lax.broadcasted_iota(jnp.int32, (QUERIES, QUERIES), 0)
        t = lax.broadcasted_iota(jnp.int32, (QUERIES, QUERIES), 1)
        last = jnp.where(u <= t, x[own - QUERIES :], -1e30)
        return jnp.concatenate([x[: own - QUERIES], last], axis=0) if own > QUERIES else last

    def weigh(unit, x):
        peak = jnp.max(x, axis=0, keepdims=True)
        return peak, jnp.exp2((x - peak) * EXPONENT_SCALE).astype(jnp.bfloat16)

    def finish(unit, held):
        h, r = unit
        peak, weight = held
        total = jnp.dot(v_t[:, : weight.shape[0]], weight, preferred_element_type=jnp.float32)
        at = slice(r * QUERIES, (r + 1) * QUERIES)
        kept_ref[h, :HD, at] = total[:HD]
        row = lax.broadcasted_iota(jnp.int32, (KEPT - HD, QUERIES), 0)
        kept_ref[h, HD:, at] = jnp.where(row == 0, total[HD : HD + KEPT - HD], peak)

    staggered(units_of(HEADS), scores, weigh, finish)


def attend_own(queries, keys, values, heads):
    steps = GROUP // HEADS
    count, first = len(heads), heads[0]
    pairs = BLOCK * BLOCK * GROUP * count
    return pl.pallas_call(
        own_kernel,
        out_shape=jax.ShapeDtypeStruct((GROUP * count, KEPT, BLOCK), jnp.float32),
        grid=(count, steps),
        in_specs=[
            pl.BlockSpec((BLOCK, HEADS * HD), lambda g, h: (0, (first + g) * steps + h)),
            pl.BlockSpec((BLOCK, HD), lambda g, h: (0, first + g)),
            pl.BlockSpec((BLOCK, HD), lambda g, h: (0, first + g)),
        ],
        out_specs=pl.BlockSpec((HEADS, KEPT, BLOCK), lambda g, h: (g * steps + h, 0, 0)),
        scratch_shapes=[pltpu.VMEM((HD + ONES, BLOCK), jnp.bfloat16)],
        cost_estimate=pl.CostEstimate(
            flops=4 * pairs * HD, transcendentals=pairs, bytes_accessed=4 * GROUP * count * KEPT * BLOCK
        ),
    )(queries, keys, values)


def slots_kernel(dead_ref, q_ref, kept_ref, ks_ref, vs_ref, *rest):
    out_ref, k_all, v_t = rest[-3:]

    @pl.when(pl.program_id(1) == 0)
    def _():
        for s in range(TOPK):
            at = slice(BLOCK * s, BLOCK * (s + 1))
            k_all[at] = ks_ref[:, s].reshape(BLOCK, HD)
            v_t[:HD, at] = vs_ref[:, s].reshape(BLOCK, HD).T
        v_t[HD:] = jnp.ones((ONES, TOPK * BLOCK), jnp.bfloat16)

    drop = [dead_ref[s] for s in range(TOPK)]
    spans = [(BLOCK * s, BLOCK * (s + 1)) for s in range(TOPK)]

    def scores(unit):
        q = q_ref[piece(unit)]
        return [lax.dot_general(k_all[a:b], q, NT, preferred_element_type=jnp.float32) for a, b in spans]

    def weigh(unit, score):
        h, r = unit
        mine = kept_ref[h, HD + 1 : HD + 2, r * QUERIES : (r + 1) * QUERIES]
        peak = mine
        for x, d in zip(score, drop):
            peak = jnp.maximum(peak, jnp.max(x, axis=0, keepdims=True) - d)
        shrink = jnp.exp2((mine - peak) * EXPONENT_SCALE)
        weights = [
            jnp.exp2((x - (peak + d)) * EXPONENT_SCALE).astype(jnp.bfloat16) for x, d in zip(score, drop)
        ]
        return shrink, weights

    def finish(unit, held):
        h, r = unit
        at = slice(r * QUERIES, (r + 1) * QUERIES)
        shrink, weights = held
        total = None
        for (a, b), weight in zip(spans, weights):
            part = jnp.dot(v_t[:, a:b], weight, preferred_element_type=jnp.float32)
            total = part if total is None else total + part
        mixture = kept_ref[h, :HD, at] * shrink + total[:HD]
        row_total = kept_ref[h, HD : HD + 1, at] * shrink + total[HD : HD + 1]
        out_ref[piece(unit)] = (mixture * (1.0 / row_total)).T.astype(jnp.bfloat16)

    staggered(units_of(HEADS), scores, weigh, finish)


def attend_slots(dead, queries, kept, arrived, heads, previous):
    sources, _, stripe, _ = arrived.shape
    count, first = len(heads), heads[0]
    steps = GROUP // HEADS
    block = (sources, TOPK, stripe, HD)
    in_specs = [
        pl.BlockSpec(memory_space=pltpu.SMEM),
        pl.BlockSpec((BLOCK, HEADS * HD), lambda g, h: (0, (first + g) * steps + h)),
        pl.BlockSpec((HEADS, KEPT, BLOCK), lambda g, h: (g * steps + h, 0, 0)),
        pl.BlockSpec(block, lambda g, h: (0, 0, 0, g)),
        pl.BlockSpec(block, lambda g, h: (0, 0, 0, count + g)),
    ]
    args = [dead, queries, kept, arrived, arrived]
    aliases = {}
    if previous is not None:
        in_specs.append(pl.BlockSpec(memory_space=pl.ANY))
        args.append(previous)
        aliases = {len(args) - 1: 0}
    pairs = BLOCK * TOPK * BLOCK * GROUP * count
    return pl.pallas_call(
        slots_kernel,
        out_shape=jax.ShapeDtypeStruct(queries.shape, jnp.bfloat16),
        grid=(count, steps),
        in_specs=in_specs,
        out_specs=pl.BlockSpec((BLOCK, HEADS * HD), lambda g, h: (0, (first + g) * steps + h)),
        scratch_shapes=[
            pltpu.VMEM((TOPK * BLOCK, HD), jnp.bfloat16),
            pltpu.VMEM((HD + ONES, TOPK * BLOCK), jnp.bfloat16),
        ],
        input_output_aliases=aliases,
        cost_estimate=pl.CostEstimate(
            flops=4 * pairs * HD, transcendentals=pairs, bytes_accessed=8 * BLOCK * HD * GROUP * count
        ),
    )(*args)


def after(x, *others):
    return lax.optimization_barrier((x, *others))[0]


def whole(queries, keys, values, selected):
    peers = lax.axis_size("peer")
    stripe = BLOCK // peers
    half, peer = lax.axis_index("half"), lax.axis_index("peer")

    def exchange(x):
        return lax.all_to_all(x, "peer", split_axis=0, concat_axis=0, tiled=True)

    def columns(x, heads):
        return x[:, heads[0] * HD : (heads[-1] + 1) * HD]

    twin = lax.ppermute(selected, "half", [(0, 1), (1, 0)])
    numbers = jnp.concatenate([selected, twin], axis=1)
    digits = jnp.concatenate([numbers // DIGIT, numbers % DIGIT], axis=1).astype(jnp.bfloat16)
    banded = []
    for at, heads in enumerate(CHUNKS):
        both = jnp.concatenate([columns(keys, heads), columns(values, heads)], axis=1)
        both = both.reshape(peers, stripe, both.shape[1])
        if at == 0:
            asked = jnp.pad(digits, ((0, 15), (0, both.shape[2] - 4 * TOPK)))
            both = jnp.concatenate([both, jnp.broadcast_to(asked, (peers, *asked.shape))], axis=1)
        banded.append(exchange(both))
    kept = []
    for heads in CHUNKS:
        kept.append(attend_own(queries, keys, values, heads))
    digits = banded[0][:, stripe, : 4 * TOPK].astype(jnp.int32)
    numbers = digits[:, : 2 * TOPK] * DIGIT + digits[:, 2 * TOPK :]
    requests = numbers[:, :TOPK]
    upper = jnp.where(half == 1, requests, numbers[:, TOPK:]).reshape(-1)
    lanes = jnp.arange(peers, dtype=jnp.int32)
    needed = jnp.any(upper[:, None] == lanes[None, :], axis=0).astype(jnp.int32)
    rank = jnp.sum(jnp.where(lanes[:, None] < lanes[None, :], needed[:, None], 0), axis=0)
    turns = jnp.sum(
        jnp.where((rank[:, None] == lanes[None, :]) & (needed[:, None] > 0), lanes[:, None], 0), axis=0
    )
    room = (peers + 1) // 2
    more = jnp.sum(needed) > room
    asked = requests.reshape(-1)
    turn = jnp.sum(jnp.where(asked[:, None] % peers == lanes[None, :], rank[None, :], 0), axis=1)
    near = asked // peers == half
    arrived = []
    first = None
    for band in banded:
        mine = band[:, :stripe]
        front = jnp.take(mine, turns[:room], axis=0, mode="clip")
        if first is not None:
            front = after(front, first)
        first = lax.ppermute(front, "half", [(0, 1)])

        def all_crossed(first, mine):
            rest = lax.ppermute(jnp.take(mine, turns[room:], axis=0, mode="clip"), "half", [(0, 1)])
            table = jnp.concatenate([first, rest, mine], axis=0)
            return jnp.take(table, jnp.where(near, peers + asked % peers, turn), axis=0, mode="clip")

        def few_crossed(first, mine):
            table = jnp.concatenate([first, mine], axis=0)
            return jnp.take(table, jnp.where(near, room + asked % peers, turn), axis=0, mode="clip")

        send = lax.cond(more, all_crossed, few_crossed, first, mine)
        arrived.append(exchange(send.reshape(peers, TOPK, *mine.shape[1:])))
    block = half * peers + peer
    dead = jnp.where(selected[0] < block, 0.0, 1e30).astype(jnp.float32)
    outputs = None
    for at, heads in enumerate(CHUNKS):
        outputs = attend_slots(dead, queries, kept[at], arrived[at], heads, outputs)
    return outputs


def solution(mesh):
    groups, ctx = mesh.devices.shape
    inner = Mesh(mesh.devices.reshape(groups, 2, ctx // 2), ("groups", "half", "peer"))
    spec = P(("groups", "half", "peer"), None)
    return jax.shard_map(whole, mesh=inner, in_specs=(spec,) * 4, out_specs=spec, check_vma=False)
```

```python
import math

import jax
import jax.numpy as jnp
from jax import lax
from jax.experimental import pallas as pl
from jax.experimental.pallas import tpu as pltpu
from jax.sharding import Mesh
from jax.sharding import PartitionSpec as P


QH = 32
KVH = 4
HD = 128
BLOCK = 512
TOPK = 2
GROUP = QH // KVH
EXPONENT_SCALE = math.log2(math.e) / math.sqrt(HD)
QUERIES = 512
ONES = 16
KEPT = HD + 8
DIGIT = 128
CHUNKS = ((0, 1), (2, 3))
HEADS = 4
SLOT_HEADS = 8
NT = (((1,), (1,)), ((), ()))


def piece(unit):
    h, r = unit
    return slice(r * QUERIES, (r + 1) * QUERIES), slice(h * HD, (h + 1) * HD)


def staggered(units, scores, weigh, finish):
    scored, weighed = {}, {}
    for at in range(len(units) + 2):
        for c in "SEA":
            if c == "S" and at < len(units):
                scored[at] = scores(units[at])
            if c == "E" and 0 <= at - 1 < len(units):
                weighed[at - 1] = weigh(units[at - 1], scored.pop(at - 1))
            if c == "A" and 0 <= at - 2 < len(units):
                finish(units[at - 2], weighed.pop(at - 2))


def units_of(heads):
    return [(h, r) for h in range(heads) for r in range(BLOCK // QUERIES)]


def own_kernel(q_ref, k_ref, v_ref, kept_ref, v_t):
    @pl.when(pl.program_id(1) == 0)
    def _():
        v_t[:HD] = v_ref[...].T
        v_t[HD:] = jnp.ones((ONES, BLOCK), jnp.bfloat16)

    def scores(unit):
        own = (unit[1] + 1) * QUERIES
        x = lax.dot_general(k_ref[:own], q_ref[piece(unit)], NT, preferred_element_type=jnp.float32)
        u = lax.broadcasted_iota(jnp.int32, (QUERIES, QUERIES), 0)
        t = lax.broadcasted_iota(jnp.int32, (QUERIES, QUERIES), 1)
        last = jnp.where(u <= t, x[own - QUERIES :], -1e30)
        return jnp.concatenate([x[: own - QUERIES], last], axis=0) if own > QUERIES else last

    def weigh(unit, x):
        peak = jnp.max(x, axis=0, keepdims=True)
        return peak, jnp.exp2((x - peak) * EXPONENT_SCALE).astype(jnp.bfloat16)

    def finish(unit, held):
        h, r = unit
        peak, weight = held
        total = jnp.dot(v_t[:, : weight.shape[0]], weight, preferred_element_type=jnp.float32)
        at = slice(r * QUERIES, (r + 1) * QUERIES)
        kept_ref[h, :HD, at] = total[:HD]
        row = lax.broadcasted_iota(jnp.int32, (KEPT - HD, QUERIES), 0)
        kept_ref[h, HD:, at] = jnp.where(row == 0, total[HD : HD + KEPT - HD], peak)

    staggered(units_of(HEADS), scores, weigh, finish)


def attend_own(queries, keys, values, heads):
    steps = GROUP // HEADS
    count, first = len(heads), heads[0]
    pairs = BLOCK * BLOCK * GROUP * count
    return pl.pallas_call(
        own_kernel,
        out_shape=jax.ShapeDtypeStruct((GROUP * count, KEPT, BLOCK), jnp.float32),
        grid=(count, steps),
        in_specs=[
            pl.BlockSpec((BLOCK, HEADS * HD), lambda g, h: (0, (first + g) * steps + h)),
            pl.BlockSpec((BLOCK, HD), lambda g, h: (0, first + g)),
            pl.BlockSpec((BLOCK, HD), lambda g, h: (0, first + g)),
        ],
        out_specs=pl.BlockSpec((HEADS, KEPT, BLOCK), lambda g, h: (g * steps + h, 0, 0)),
        scratch_shapes=[pltpu.VMEM((HD + ONES, BLOCK), jnp.bfloat16)],
        cost_estimate=pl.CostEstimate(
            flops=4 * pairs * HD, transcendentals=pairs, bytes_accessed=4 * GROUP * count * KEPT * BLOCK
        ),
    )(queries, keys, values)


def slots_kernel(dead_ref, q_ref, kept_ref, ks_ref, vs_ref, *rest):
    out_ref, k_all, v_t = rest[-3:]

    @pl.when(pl.program_id(1) == 0)
    def _():
        for s in range(TOPK):
            at = slice(BLOCK * s, BLOCK * (s + 1))
            k_all[at] = ks_ref[:, s].reshape(BLOCK, HD)
            v_t[:HD, at] = vs_ref[:, s].reshape(BLOCK, HD).T
        v_t[HD:] = jnp.ones((ONES, TOPK * BLOCK), jnp.bfloat16)

    drop = [dead_ref[s] for s in range(TOPK)]
    spans = [(BLOCK * s, BLOCK * (s + 1)) for s in range(TOPK)]

    def scores(unit):
        q = q_ref[piece(unit)]
        return [lax.dot_general(k_all[a:b], q, NT, preferred_element_type=jnp.float32) for a, b in spans]

    def weigh(unit, score):
        h, r = unit
        mine = kept_ref[h, HD + 1 : HD + 2, r * QUERIES : (r + 1) * QUERIES]
        peak = mine
        for x, d in zip(score, drop):
            peak = jnp.maximum(peak, jnp.max(x, axis=0, keepdims=True) - d)
        shrink = jnp.exp2((mine - peak) * EXPONENT_SCALE)
        weights = [
            jnp.exp2((x - (peak + d)) * EXPONENT_SCALE).astype(jnp.bfloat16) for x, d in zip(score, drop)
        ]
        return shrink, weights

    def finish(unit, held):
        h, r = unit
        at = slice(r * QUERIES, (r + 1) * QUERIES)
        shrink, weights = held
        total = None
        for (a, b), weight in zip(spans, weights):
            part = jnp.dot(v_t[:, a:b], weight, preferred_element_type=jnp.float32)
            total = part if total is None else total + part
        mixture = kept_ref[h, :HD, at] * shrink + total[:HD]
        row_total = kept_ref[h, HD : HD + 1, at] * shrink + total[HD : HD + 1]
        out_ref[piece(unit)] = (mixture * (1.0 / row_total)).T.astype(jnp.bfloat16)

    staggered(units_of(SLOT_HEADS), scores, weigh, finish)


def attend_slots(dead, queries, kept, arrived, heads, previous):
    sources, _, stripe, _ = arrived.shape
    count, first = len(heads), heads[0]
    steps = GROUP // SLOT_HEADS
    block = (sources, TOPK, stripe, HD)
    in_specs = [
        pl.BlockSpec(memory_space=pltpu.SMEM),
        pl.BlockSpec((BLOCK, SLOT_HEADS * HD), lambda g, h: (0, (first + g) * steps + h)),
        pl.BlockSpec((SLOT_HEADS, KEPT, BLOCK), lambda g, h: (g * steps + h, 0, 0)),
        pl.BlockSpec(block, lambda g, h: (0, 0, 0, g)),
        pl.BlockSpec(block, lambda g, h: (0, 0, 0, count + g)),
    ]
    args = [dead, queries, kept, arrived, arrived]
    aliases = {}
    if previous is not None:
        in_specs.append(pl.BlockSpec(memory_space=pl.ANY))
        args.append(previous)
        aliases = {len(args) - 1: 0}
    pairs = BLOCK * TOPK * BLOCK * GROUP * count
    return pl.pallas_call(
        slots_kernel,
        out_shape=jax.ShapeDtypeStruct(queries.shape, jnp.bfloat16),
        grid=(count, steps),
        in_specs=in_specs,
        out_specs=pl.BlockSpec((BLOCK, SLOT_HEADS * HD), lambda g, h: (0, (first + g) * steps + h)),
        scratch_shapes=[
            pltpu.VMEM((TOPK * BLOCK, HD), jnp.bfloat16),
            pltpu.VMEM((HD + ONES, TOPK * BLOCK), jnp.bfloat16),
        ],
        input_output_aliases=aliases,
        cost_estimate=pl.CostEstimate(
            flops=4 * pairs * HD, transcendentals=pairs, bytes_accessed=8 * BLOCK * HD * GROUP * count
        ),
    )(*args)


def after(x, *others):
    return lax.optimization_barrier((x, *others))[0]


def whole(queries, keys, values, selected):
    peers = lax.axis_size("peer")
    stripe = BLOCK // peers
    half, peer = lax.axis_index("half"), lax.axis_index("peer")

    def exchange(x):
        return lax.all_to_all(x, "peer", split_axis=0, concat_axis=0, tiled=True)

    def columns(x, heads):
        return x[:, heads[0] * HD : (heads[-1] + 1) * HD]

    twin = lax.ppermute(selected, "half", [(0, 1), (1, 0)])
    numbers = jnp.concatenate([selected, twin], axis=1)
    digits = jnp.concatenate([numbers // DIGIT, numbers % DIGIT], axis=1).astype(jnp.bfloat16)
    banded = []
    for at, heads in enumerate(CHUNKS):
        both = jnp.concatenate([columns(keys, heads), columns(values, heads)], axis=1)
        both = both.reshape(peers, stripe, both.shape[1])
        if at == 0:
            asked = jnp.pad(digits, ((0, 15), (0, both.shape[2] - 4 * TOPK)))
            both = jnp.concatenate([both, jnp.broadcast_to(asked, (peers, *asked.shape))], axis=1)
        banded.append(exchange(both))
    kept = []
    for heads in CHUNKS:
        kept.append(attend_own(queries, keys, values, heads))
    digits = banded[0][:, stripe, : 4 * TOPK].astype(jnp.int32)
    numbers = digits[:, : 2 * TOPK] * DIGIT + digits[:, 2 * TOPK :]
    requests = numbers[:, :TOPK]
    upper = jnp.where(half == 1, requests, numbers[:, TOPK:]).reshape(-1)
    lanes = jnp.arange(peers, dtype=jnp.int32)
    needed = jnp.any(upper[:, None] == lanes[None, :], axis=0).astype(jnp.int32)
    rank = jnp.sum(jnp.where(lanes[:, None] < lanes[None, :], needed[:, None], 0), axis=0)
    turns = jnp.sum(
        jnp.where((rank[:, None] == lanes[None, :]) & (needed[:, None] > 0), lanes[:, None], 0), axis=0
    )
    room = (peers + 1) // 2
    more = jnp.sum(needed) > room
    asked = requests.reshape(-1)
    turn = jnp.sum(jnp.where(asked[:, None] % peers == lanes[None, :], rank[None, :], 0), axis=1)
    near = asked // peers == half
    arrived = []
    first = None
    for band in banded:
        mine = band[:, :stripe]
        front = jnp.take(mine, turns[:room], axis=0, mode="clip")
        if first is not None:
            front = after(front, first)
        first = lax.ppermute(front, "half", [(0, 1)])

        def all_crossed(first, mine):
            rest = lax.ppermute(jnp.take(mine, turns[room:], axis=0, mode="clip"), "half", [(0, 1)])
            table = jnp.concatenate([first, rest, mine], axis=0)
            return jnp.take(table, jnp.where(near, peers + asked % peers, turn), axis=0, mode="clip")

        def few_crossed(first, mine):
            table = jnp.concatenate([first, mine], axis=0)
            return jnp.take(table, jnp.where(near, room + asked % peers, turn), axis=0, mode="clip")

        send = lax.cond(more, all_crossed, few_crossed, first, mine)
        arrived.append(exchange(send.reshape(peers, TOPK, *mine.shape[1:])))
    block = half * peers + peer
    dead = jnp.where(selected[0] < block, 0.0, 1e30).astype(jnp.float32)
    outputs = None
    for at, heads in enumerate(CHUNKS):
        outputs = attend_slots(dead, queries, kept[at], arrived[at], heads, outputs)
    return outputs


def solution(mesh):
    groups, ctx = mesh.devices.shape
    inner = Mesh(mesh.devices.reshape(groups, 2, ctx // 2), ("groups", "half", "peer"))
    spec = P(("groups", "half", "peer"), None)
    return jax.shard_map(whole, mesh=inner, in_specs=(spec,) * 4, out_specs=spec, check_vma=False)
```
